512 devices in a mesh: seg: 8 (over x, core), blk: 64 (over y, z).
Axes of the slice: x: 4, y: 4, z: 16, core: 2. Of those that a mesh axis runs over, the one named last changes fastest.
Arguments:
- products: bfloat16 [8, 4096, 16384], P('seg', 'blk'), may hold values from -0.09375 to 0.09375
- compat: int32 [8, 64, 16], P('seg', 'blk'), may hold values 0 or 1
- sizes: int32 [8, 64], P('seg', 'blk'), may hold values from 1 to 256, 12288 in all within a row
Outputs:
- orthonormal: bfloat16 [8, 4096, 16384], P('seg', None, 'blk')
- accumulated: float32 [8, 64, 256, 256], P('seg', 'blk')
The draws below stay inside these ranges and needn't reach their ends.
Inputs may be any that keep to these rules, and one draw needn't show every extreme that they name: Each site's 64 sector sizes sum to 12288 and one of them is exactly 256.
All inputs are finite; a program needn't handle non-finite values. No bound on the sum of `compat` or of `sizes` on one device may be relied on, other than what follows from the above.
Results may differ from the reference program's by a relative error of at most 0.001.
Values may be sent and summed in bfloat16 or wider, within the bound.
A program may use at most 64 MiB of HBM per device.

```python
import math
import jax
import jax.numpy as jnp
import numpy as np
from jax import lax

W = 16
B = 256
SECT = 64
SITES = 8


def with_ends(array, rng, smallest, high):
    longest = array.shape.index(max(array.shape))
    spots = []
    for shift in (0, 1):
        where = [jax.random.randint(jax.random.fold_in(rng, axis), (), 0, length) for axis, length in enumerate(array.shape)]
        where[longest] = (where[longest] + shift) % array.shape[longest]
        spots.append(tuple(where))
    return array.at[spots[0]].set(smallest).at[spots[1]].set(high)


def block_scale(own_key, extent, cuts, smallest, high):
    loudness = 1.0
    for axis_at, parts in cuts:
        draws = jax.random.uniform(jax.random.fold_in(jax.random.fold_in(own_key, 6), axis_at), (parts,), jnp.float32, smallest / len(cuts), high / len(cuts))
        loudness = loudness * jnp.repeat(jnp.exp(draws), extent[axis_at] // parts).reshape((-1,) + (1,) * (len(extent) - 1 - axis_at))
    return loudness


def profile(amount, total, most, slope):
    portions = [(1 << 20) // math.isqrt(grade ** slope) + 1 for grade in range(2, amount + 1)]
    surplus, counts = total - most - (amount - 1), [1] * (amount - 1)
    while surplus > 0:
        movable = [i for i in range(amount - 1) if counts[i] < most]
        pool, remaining = sum([portions[i] for i in movable]), surplus
        for i in movable:
            addition = min(most - counts[i], max(1, remaining * portions[i] // pool), surplus)
            counts[i] = counts[i] + addition
            surplus = surplus - addition
    return np.array([most] + counts)


def ragged(key, amount, total, limit, slope):
    if amount == 2:
        one = jax.random.randint(key, (), max(1, total - limit), min(limit, total - 1) + 1)
        return jnp.stack([one, total - one])
    sizes = jnp.asarray(profile(amount, total, limit, slope), jnp.int32)
    couples = (amount - 1) // 2
    giver, sink = sizes[1:1 + 2 * couples:2], sizes[2:2 + 2 * couples:2]
    margin = jnp.minimum(giver - 1, limit - sink)
    shifted = jax.random.randint(jax.random.fold_in(key, 1), (couples,), 0, 1 << 20) % (margin + 1)
    sizes = sizes.at[1:1 + 2 * couples:2].set(giver - shifted).at[2:2 + 2 * couples:2].set(sink + shifted)
    return sizes[jax.random.permutation(jax.random.fold_in(key, 2), amount)]


def gaussian(own_key, dims, spread, reach, cuts=(), kind=jnp.bfloat16):
    drawn = spread * jax.random.normal(own_key, dims, jnp.float32)
    if cuts:
        drawn = drawn * block_scale(own_key, dims, cuts, -0.22, 0.18)
    return jnp.clip(drawn, -reach, reach).astype(kind)


def setup_inputs(seed: int = 0) -> dict:
    arg_keys = jax.random.split(jax.random.key(seed), 4)
    return {
        "products": gaussian(arg_keys[0], (SITES, W * B, SECT * B), (W * B) ** -0.5, 0.09375, ((0, 8), (1, 64))),
        "compat": with_ends((jax.random.randint(arg_keys[1], (SITES, SECT, W), 0, 4) < 3).astype(jnp.int32), jax.random.fold_in(arg_keys[1], 1), 0, 1),
        "sizes": jax.vmap(lambda own: ragged(own, SECT, 3 * SECT * B // 4, B, 2))(jax.random.split(arg_keys[2], SITES)).reshape((SITES, SECT)).astype(jnp.int32),
    }


shift_value = 0.05

def factor_sector(panel_in, allowed, live_cols):
    total_rows = panel_in.shape[0]
    width_cols = panel_in.shape[1]
    gate_rows = jnp.repeat(allowed, total_rows // allowed.shape[0], total_repeat_length=total_rows).astype(jnp.bfloat16)
    masked = panel_in * gate_rows[:, None] * live_cols.astype(jnp.bfloat16)[None, :]
    gram_raw = jnp.dot(masked.T.astype(jnp.float32), masked.astype(jnp.float32), preferred_element_type=jnp.float32)
    identity = jnp.eye(width_cols, dtype=jnp.float32)
    lower_one = jnp.linalg.cholesky(gram_raw + shift_value * identity)
    first_t = jax.scipy.linalg.solve_triangular(lower_one, masked.astype(jnp.float32).T, lower=True)
    gram_two = jnp.dot(first_t, first_t.T, precision=lax.Precision.HIGHEST) + shift_value * identity
    lower_two = jnp.linalg.cholesky(gram_two)
    ortho_t = jax.scipy.linalg.solve_triangular(lower_two, first_t, lower=True)
    factor_r = jnp.dot(lower_two.T, lower_one.T, precision=lax.Precision.HIGHEST)
    return (ortho_t.T.astype(jnp.bfloat16), factor_r)

def reference(products, compat, sizes):
    columns = jnp.arange(B, dtype=jnp.int32)
    live = (columns[None, None, :] < sizes[:, :, None]).astype(jnp.int32)

    def per_sector(sector):
        start = (sector * B).astype(jnp.int32)
        panels = lax.dynamic_slice_in_dim(products, start, B, 2)
        allowed = lax.dynamic_index_in_dim(compat, sector, 1, keepdims=False)
        live_now = lax.dynamic_index_in_dim(live, sector, 1, keepdims=False)
        return jax.vmap(factor_sector)(panels, allowed, live_now)
    ortho_all, factor_all = lax.map(per_sector, jnp.arange(SECT, dtype=jnp.int32))
    orthonormal = ortho_all.transpose(1, 2, 0, 3).reshape(SITES, W * B, SECT * B)
    factor_sites = factor_all.transpose(1, 0, 2, 3)

    def advance(carry, factor_now):
        updated = jnp.einsum('kab,kbc->kac', factor_now, carry, precision=lax.Precision.HIGHEST)
        return (updated, updated)
    start_carry = jnp.broadcast_to(jnp.eye(B, dtype=jnp.float32), (SECT, B, B))
    _, accumulated = lax.scan(advance, start_carry, factor_sites)
    return (orthonormal, accumulated)
```

```python
import jax
import jax.numpy as jnp
from jax import lax
from jax.experimental import pallas as pl
from jax.experimental.pallas import tpu as pltpu
from jax.sharding import PartitionSpec as P

B = 256
H = 128
ROWS = 64
NY, NZ = 4, 16
NB = 8
shift_value = 0.05
MESH = pl.DeviceIdType.MESH
HI = lax.Precision.HIGHEST
F32, BF16 = jnp.float32, jnp.bfloat16


def split3(x):
    a = x.astype(BF16)
    rest = x - a.astype(F32)
    b = rest.astype(BF16)
    return a, b, (rest - b.astype(F32)).astype(BF16)


def transposed_dot(x, y):
    xa, xb, xc = split3(x)
    ya, yb, yc = split3(y)
    left = jnp.concatenate([xa, xb, xa, xc, xa, xb], 0)
    right = jnp.concatenate([ya, ya, yb, ya, yc, yb], 0)
    return lax.dot_general(left, right, (((0,), (0,)), ((), ())), preferred_element_type=F32)


def dot_hi(x, y):
    return jnp.dot(x, y, precision=HI, preferred_element_type=F32)


def eliminate(w, v, base):
    row = lax.broadcasted_iota(jnp.int32, (NB, H), 0)
    cols = [jnp.broadcast_to(w[:, base + k : base + k + 1], (NB, H)) for k in range(NB)]
    pivots = jnp.zeros((NB, H), F32)
    for c in range(NB):
        p = jnp.broadcast_to(cols[c][c : c + 1, :], (NB, H))
        pivots = jnp.where(row == c, p, pivots)
        if c == NB - 1:
            break
        m = jnp.where(row > c, cols[c] * (1.0 / p), 0.0)
        for k in range(c + 1, NB):
            cols[k] = cols[k] - m * jnp.broadcast_to(cols[k][c : c + 1, :], (NB, H))
        w = w - m * jnp.broadcast_to(w[c : c + 1, :], (NB, H))
        v = v - m * jnp.broadcast_to(v[c : c + 1, :], (NB, H))
    root = lax.rsqrt(pivots)
    return w * root, v * root


def cholesky(work):
    work[:, H:] = (lax.broadcasted_iota(jnp.int32, (H, H), 0) == lax.broadcasted_iota(jnp.int32, (H, H), 1)).astype(F32)
    lane = lax.broadcasted_iota(jnp.int32, (NB, H), 1)
    row = lax.broadcasted_iota(jnp.int32, (NB, H), 0)
    for start in range(0, H, NB):
        end = start + NB
        r, v = eliminate(work[start:end, :H], work[start:end, H:], start)
        r = jnp.where(lane >= row + start, r, 0.0)
        rv = jnp.concatenate([r, v], 1)
        work[start:end, :] = rv
        if end < H:
            work[end:, :] = work[end:, :] - transposed_dot(r, rv)[end:, :]


def kernel(x, compat, sizes, q_out, acc_out, pa, pb, qa, qb, w1, w2, r_own, r_pair, pairs, c_all,
           send_sem, recv_sem, own_sem, wave_sem, out_sem, pair_send, pair_recv, ring_send, ring_recv, swap_send, swap_recv):
    b = lax.axis_index("blk")
    s = lax.axis_index("seg")
    y, z = b // NZ, lax.rem(b, NZ)
    chip, core = s // 2, lax.rem(s, 2)
    mate = chip * 2 + 1 - core
    panels = (pa, pb)

    def at(dy, dz):
        return lax.rem(y + dy, NY) * NZ + lax.rem(z + dz + NZ, NZ)

    def rows_of(k):
        return pl.ds(pl.multiple_of(k * ROWS, ROWS), ROWS)

    barrier = pltpu.get_barrier_semaphore()
    near = [{"blk": at(dy, 0)} for dy in (1, 2, 3)] + [{"blk": at(0, 1)}, {"blk": at(0, -1)}]
    near += [{"seg": mate}] + [{"seg": lax.rem(chip + d, 4) * 2 + core} for d in (1, 2, 3)]
    for to in near:
        pl.semaphore_signal(barrier, inc=1, device_id=to, device_id_type=MESH)
    pl.semaphore_wait(barrier, len(near))

    def send(half, dy, dz):
        k = at(dy, dz)
        return pltpu.make_async_remote_copy(
            src_ref=x.at[:, pl.ds(pl.multiple_of(k * B + half * H, H), H)],
            dst_ref=panels[half].at[rows_of(b), :],
            send_sem=send_sem.at[half],
            recv_sem=recv_sem.at[half, dz % NZ, dy],
            device_id={"blk": k},
            device_id_type=MESH,
        )

    def arrived(half, dy, dz):
        k = at(NY - dy, -dz)
        pltpu.make_async_remote_copy(
            src_ref=x.at[:, pl.ds(0, H)],
            dst_ref=panels[half].at[rows_of(k), :],
            send_sem=send_sem.at[half],
            recv_sem=recv_sem.at[half, dz % NZ, dy],
            device_id={"blk": k},
            device_id_type=MESH,
        ).wait_recv()

    own = [
        pltpu.make_async_copy(
            x.at[:, pl.ds(pl.multiple_of(b * B + half * H, H), H)], panels[half].at[rows_of(b), :], own_sem.at[half]
        )
        for half in (0, 1)
    ]
    own[0].start()
    own[1].start()

    def tell(direction, hop):
        pl.semaphore_signal(
            wave_sem.at[(1 - direction) // 2, hop - 1],
            inc=1,
            device_id={"blk": at(0, direction)},
            device_id_type=MESH,
        )

    tell(1, 1)
    tell(-1, 1)
    for dy in (1, 2, 3):
        send(0, dy, 0).start()
    for hop in range(1, 9):
        for direction in (1, -1):
            if hop == 8 and direction == -1:
                continue
            pl.semaphore_wait(wave_sem.at[(1 + direction) // 2, hop - 1], 1)
            if hop < 7 or (hop == 7 and direction == 1):
                tell(-direction, hop + 1)
            for dy in range(4):
                send(0, dy, direction * hop).start()
    order_b = [8] + [d * sign for d in range(7, 0, -1) for sign in (1, -1)]
    for dz in order_b:
        for dy in range(4):
            send(1, dy, dz).start()
    for dy in (1, 2, 3):
        send(1, dy, 0).start()

    n = sizes[0, 0]
    lane = lax.broadcasted_iota(jnp.int32, (H, H), 1)
    row = lax.broadcasted_iota(jnp.int32, (H, H), 0)
    live_row = [(row < n).astype(F32), (row + H < n).astype(F32)]
    live_lane = [(lane < n).astype(F32), (lane + H < n).astype(F32)]

    def collect(half, dz):
        zs = lax.rem(z - dz + NZ, NZ)
        if dz == 0:
            own[half].wait()
        for dy in range(4):
            if dy or dz:
                arrived(half, dy, dz)
        parts = []
        for ys in range(4):
            k = ys * NZ + zs
            gate = jnp.full((1, H), compat[0, ys * 4 + zs // 4], jnp.int32).astype(F32).astype(BF16)
            part = panels[half][rows_of(k), :] * gate
            panels[half][rows_of(k), :] = part
            parts.append(part)
        return jnp.concatenate(parts, 0)

    def other(dz):
        zs = lax.rem(z - dz + NZ, NZ)
        return jnp.concatenate([pa[rows_of(ys * NZ + zs), :] for ys in range(4)], 0)

    def gram(left, right):
        return lax.dot_general(left, right, (((0,), (0,)), ((), ())), preferred_element_type=F32)

    w1[:, :H] = jnp.zeros((H, H), F32)
    for dz in [0] + [d * sign for d in range(1, 8) for sign in (1, -1)] + [8]:
        part = collect(0, dz)
        w1[:, :H] += gram(part, part)
    shifted = (row == lane).astype(F32) * (shift_value * shift_value)
    w1[:, :H] = w1[:, :H] * (live_row[0] * live_lane[0] * (1.0 + shift_value)) + shifted
    cholesky(w1)
    t11 = w1[:, H:].T
    r_own[:H, :H] = w1[:, :H]
    r_own[H:, :H] = jnp.zeros((H, H), F32)

    def both(t):
        high = t.astype(BF16)
        return jnp.concatenate([high, (t - high.astype(F32)).astype(BF16)], 1)

    t1 = both(t11 * live_row[0])

    def first_columns(i, _):
        at_rows = pl.ds(pl.multiple_of(i * B, B), B)
        out = jnp.dot(pa[at_rows, :], t1, preferred_element_type=F32)
        qa[at_rows, :] = (out[:, :H] + out[:, H:]).astype(BF16)
        return 0

    lax.fori_loop(0, 16, first_columns, 0)
    write_a = pltpu.make_async_copy(qa, q_out.at[:, pl.ds(0, H)], out_sem.at[0])
    write_a.start()

    r_own[:H, H:] = jnp.zeros((H, H), F32)
    w2[:, :H] = jnp.zeros((H, H), F32)
    for dz in order_b + [0]:
        part = collect(1, dz)
        r_own[:H, H:] += gram(other(dz), part)
        w2[:, :H] += gram(part, part)
    a12 = r_own[:H, H:] * (live_row[0] * live_lane[1] * (1.0 + shift_value))
    a22 = w2[:, :H] * (live_row[1] * live_lane[1] * (1.0 + shift_value)) + shifted
    r12 = dot_hi(w1[:, H:], a12)
    r_own[:H, H:] = r12
    w2[:, :H] = a22 - transposed_dot(r12, r12)
    mixed = dot_hi(t11, r12)
    cholesky(w2)
    r_own[H:, H:] = w2[:, :H]
    to_mate = pltpu.make_async_remote_copy(
        src_ref=r_own, dst_ref=r_pair, send_sem=pair_send, recv_sem=pair_recv, device_id={"seg": mate}, device_id_type=MESH
    )
    to_mate.start()

    t22 = w2[:, H:].T
    t12 = dot_hi(mixed, t22)
    t2 = both(jnp.concatenate([-t12 * live_row[0], t22 * live_row[1]], 0))

    def last_columns(i, _):
        at_rows = pl.ds(pl.multiple_of(i * B, B), B)
        out = jnp.dot(jnp.concatenate([pa[at_rows, :], pb[at_rows, :]], 1), t2, preferred_element_type=F32)
        qb[at_rows, :] = (out[:, :H] + out[:, H:]).astype(BF16)
        return 0

    lax.fori_loop(0, 8, last_columns, 0)

    to_mate.wait()
    is_even = core == 0
    later = jnp.where(is_even, r_pair[...], r_own[...])
    earlier = jnp.where(is_even, r_own[...], r_pair[...])
    pairs[...] = dot_hi(later, earlier)
    half_rows = pl.ds(pl.multiple_of(core * H, H), H)
    ring = []
    for d in (1, 2, 3):
        copy = pltpu.make_async_remote_copy(
            src_ref=pairs.at[half_rows, :],
            dst_ref=c_all.at[chip, half_rows, :],
            send_sem=ring_send.at[d - 1],
            recv_sem=ring_recv.at[d - 1],
            device_id={"seg": lax.rem(chip + d, 4) * 2 + core},
            device_id_type=MESH,
        )
        copy.start()
        ring.append(copy)
    lax.fori_loop(8, 16, last_columns, 0)
    write_b = pltpu.make_async_copy(qb, q_out.at[:, pl.ds(H, H)], out_sem.at[1])
    write_b.start()
    swaps = []
    for d in (1, 2, 3):
        source = lax.rem(chip + 4 - d, 4)
        ring[d - 1].wait()
        copy = pltpu.make_async_remote_copy(
            src_ref=c_all.at[source, half_rows, :],
            dst_ref=c_all.at[source, half_rows, :],
            send_sem=swap_send.at[d - 1],
            recv_sem=swap_recv.at[d - 1],
            device_id={"seg": mate},
            device_id_type=MESH,
        )
        copy.start()
        swaps.append(copy)
    for copy in swaps:
        copy.wait()
    mine = jnp.where(is_even, r_own[...], pairs[...])

    @pl.when(chip == 0)
    def _():
        acc_out[...] = mine

    @pl.when(chip > 0)
    def _():
        before = lax.fori_loop(1, chip, lambda i, e: dot_hi(c_all[i], e), c_all[0])
        acc_out[...] = dot_hi(mine, before)

    for half in (0, 1):
        pltpu.make_async_remote_copy(
            src_ref=x.at[:, pl.ds(0, 63 * H)],
            dst_ref=x.at[:, pl.ds(0, 63 * H)],
            send_sem=send_sem.at[half],
            recv_sem=recv_sem.at[half, 0, 0],
            device_id={"blk": b},
            device_id_type=MESH,
        ).wait_send()
    write_a.wait()
    write_b.wait()


def local(products, compat, sizes):
    vmem, dma = pltpu.VMEM, pltpu.SemaphoreType.DMA
    ortho, acc = pl.pallas_call(
        kernel,
        out_shape=(jax.ShapeDtypeStruct((NY * NZ * ROWS, B), BF16), jax.ShapeDtypeStruct((B, B), F32)),
        in_specs=[
            pl.BlockSpec(memory_space=pl.ANY),
            pl.BlockSpec(memory_space=pltpu.SMEM),
            pl.BlockSpec(memory_space=pltpu.SMEM),
        ],
        out_specs=(pl.BlockSpec(memory_space=pl.ANY), pl.BlockSpec(memory_space=pltpu.VMEM)),
        scratch_shapes=[vmem((NY * NZ * ROWS, H), BF16)] * 4
        + [vmem((H, B), F32)] * 2
        + [vmem((B, B), F32)] * 3
        + [vmem((4, B, B), F32)]
        + [
            dma((2,)),
            dma((2, NZ, NY)),
            dma((2,)),
            pltpu.SemaphoreType.REGULAR((2, 8)),
            dma((2,)),
            dma,
            dma,
            dma((3,)),
            dma((3,)),
            dma((3,)),
            dma((3,)),
        ],
        compiler_params=pltpu.CompilerParams(collective_id=0, has_side_effects=True, vmem_limit_bytes=40 << 20),
        name="sweep",
    )(products[0], compat[0], sizes)
    return ortho[None], acc[None, None]


def solution(mesh):
    in_specs = (P("seg", "blk", None), P("seg", "blk", None), P("seg", "blk"))
    out_specs = (P("seg", None, "blk"), P("seg", "blk", None, None))
    return jax.shard_map(local, mesh=mesh, in_specs=in_specs, out_specs=out_specs, check_vma=False)
```

```python
import jax
import jax.numpy as jnp
from jax import lax
from jax.experimental import pallas as pl
from jax.experimental.pallas import tpu as pltpu
from jax.sharding import PartitionSpec as P

B = 256
H = 128
ROWS = 64
NY, NZ = 4, 16
NB = 8
SUPER = 32
shift_value = 0.05
MESH = pl.DeviceIdType.MESH
HI = lax.Precision.HIGHEST
F32, BF16 = jnp.float32, jnp.bfloat16


def split3(x):
    a = x.astype(BF16)
    rest = x - a.astype(F32)
    b = rest.astype(BF16)
    return a, b, (rest - b.astype(F32)).astype(BF16)


def transposed_dot(x, y):
    xa, xb, xc = split3(x)
    ya, yb, yc = split3(y)
    left = jnp.concatenate([xa, xb, xa, xc, xa, xb], 0)
    right = jnp.concatenate([ya, ya, yb, ya, yc, yb], 0)
    return lax.dot_general(left, right, (((0,), (0,)), ((), ())), preferred_element_type=F32)


def dot_hi(x, y):
    return jnp.dot(x, y, precision=HI, preferred_element_type=F32)


def spread(x, r):
    return jnp.broadcast_to(x[r : r + 1, :], (NB, H))


def eliminate(w, v, base):
    groups = len(w)
    row = lax.broadcasted_iota(jnp.int32, (NB, H), 0)
    for g in range(groups):
        first = base + NB * g
        cols = [[jnp.broadcast_to(w[h][:, first + k : first + k + 1], (NB, H)) for k in range(NB)] for h in range(g, groups)]
        pivots = jnp.zeros((NB, H), F32)
        for c in range(NB):
            p = spread(cols[0][c], c)
            pivots = jnp.where(row == c, p, pivots)
            if c == NB - 1 and g == groups - 1:
                break
            q = 1.0 / p
            m = [cols[h - g][c] * q for h in range(g, groups)]
            m[0] = jnp.where(row > c, m[0], 0.0)
            for k in range(c + 1, NB):
                along = spread(cols[0][k], c)
                for h in range(g, groups):
                    cols[h - g][k] = cols[h - g][k] - m[h - g] * along
            w_row, v_row = spread(w[g], c), spread(v[g], c)
            for h in range(g + (c == NB - 1), groups):
                w[h] = w[h] - m[h - g] * w_row
                v[h] = v[h] - m[h - g] * v_row
        root = lax.rsqrt(pivots)
        w[g] = w[g] * root
        v[g] = v[g] * root
    return w, v


def cholesky(work):
    work[:, H:] = (lax.broadcasted_iota(jnp.int32, (H, H), 0) == lax.broadcasted_iota(jnp.int32, (H, H), 1)).astype(F32)
    lane = lax.broadcasted_iota(jnp.int32, (SUPER, H), 1)
    row = lax.broadcasted_iota(jnp.int32, (SUPER, H), 0)
    for start in range(0, H, SUPER):
        end = start + SUPER
        pieces = range(start, end, NB)
        w, v = eliminate([work[i : i + NB, :H] for i in pieces], [work[i : i + NB, H:] for i in pieces], start)
        r = jnp.where(lane >= row + start, jnp.concatenate(w, 0), 0.0)
        rv = jnp.concatenate([r, jnp.concatenate(v, 0)], 1)
        work[start:end, :] = rv
        if end < H:
            work[end:, :] = work[end:, :] - transposed_dot(r, rv)[end:, :]


def kernel(x, compat_in, sizes_in, q_out, acc_out, pa, pb, qa, qb, w1, w2, c_all, pairs, run,
           send_sem, recv_sem, own_sem, wave_sem, out_sem, mate_send, mate_recv, ring_send, ring_recv, swap_send, swap_recv,
           compat, sizes, table_sem):
    b = lax.axis_index("blk")
    s = lax.axis_index("seg")
    y, z = b // NZ, lax.rem(b, NZ)
    chip, core = s // 2, lax.rem(s, 2)
    mate = chip * 2 + 1 - core
    panels = (pa, pb)

    def at(dy, dz):
        return lax.rem(y + dy, NY) * NZ + lax.rem(z + dz + NZ, NZ)

    def rows_of(k):
        return pl.ds(pl.multiple_of(k * ROWS, ROWS), ROWS)

    tables = [
        pltpu.make_async_copy(compat_in, compat, table_sem.at[0]),
        pltpu.make_async_copy(sizes_in, sizes, table_sem.at[1]),
    ]
    for copy in tables:
        copy.start()

    barrier = pltpu.get_barrier_semaphore()
    near = [{"blk": at(dy, 0)} for dy in (1, 2, 3)] + [{"blk": at(0, 1)}, {"blk": at(0, -1)}]
    near += [{"seg": mate}] + [{"seg": lax.rem(chip + d, 4) * 2 + core} for d in (1, 2, 3)]
    for to in near:
        pl.semaphore_signal(barrier, inc=1, device_id=to, device_id_type=MESH)
    pl.semaphore_wait(barrier, len(near))

    def send(half, dy, dz):
        k = at(dy, dz)
        return pltpu.make_async_remote_copy(
            src_ref=x.at[:, pl.ds(pl.multiple_of(k * B + half * H, H), H)],
            dst_ref=panels[half].at[rows_of(b), :],
            send_sem=send_sem.at[half],
            recv_sem=recv_sem.at[half, dz % NZ, dy],
            device_id={"blk": k},
            device_id_type=MESH,
        )

    def arrived(half, dy, dz):
        k = at(NY - dy, -dz)
        pltpu.make_async_remote_copy(
            src_ref=x.at[:, pl.ds(0, H)],
            dst_ref=panels[half].at[rows_of(k), :],
            send_sem=send_sem.at[half],
            recv_sem=recv_sem.at[half, dz % NZ, dy],
            device_id={"blk": k},
            device_id_type=MESH,
        ).wait_recv()

    own = [
        pltpu.make_async_copy(
            x.at[:, pl.ds(pl.multiple_of(b * B + half * H, H), H)], panels[half].at[rows_of(b), :], own_sem.at[half]
        )
        for half in (0, 1)
    ]
    own[0].start()
    own[1].start()

    def tell(direction, hop):
        pl.semaphore_signal(
            wave_sem.at[(1 - direction) // 2, hop - 1],
            inc=1,
            device_id={"blk": at(0, direction)},
            device_id_type=MESH,
        )

    tell(1, 1)
    tell(-1, 1)
    for dy in (1, 2, 3):
        send(0, dy, 0).start()
    for hop in range(1, 9):
        for direction in (1, -1):
            if hop == 8 and direction == -1:
                continue
            pl.semaphore_wait(wave_sem.at[(1 + direction) // 2, hop - 1], 1)
            if hop < 7 or (hop == 7 and direction == 1):
                tell(-direction, hop + 1)
            for dy in range(4):
                send(0, dy, direction * hop).start()
    order_b = [8] + [d * sign for d in range(7, 0, -1) for sign in (1, -1)]
    for dz in order_b:
        for dy in range(4):
            send(1, dy, dz).start()
    for dy in (1, 2, 3):
        send(1, dy, 0).start()

    for copy in tables:
        copy.wait()
    n = sizes[0, 0]
    lane = lax.broadcasted_iota(jnp.int32, (H, H), 1)
    row = lax.broadcasted_iota(jnp.int32, (H, H), 0)
    live_row = [(row < n).astype(F32), (row + H < n).astype(F32)]
    live_lane = [(lane < n).astype(F32), (lane + H < n).astype(F32)]

    def collect(half, dz):
        zs = lax.rem(z - dz + NZ, NZ)
        if dz == 0:
            own[half].wait()
        for dy in range(4):
            if dy or dz:
                arrived(half, dy, dz)
        parts = []
        for ys in range(4):
            k = ys * NZ + zs
            gate = jnp.full((1, H), compat[0, ys * 4 + zs // 4], jnp.int32).astype(F32).astype(BF16)
            part = panels[half][rows_of(k), :] * gate
            panels[half][rows_of(k), :] = part
            parts.append(part)
        return jnp.concatenate(parts, 0)

    def other(dz):
        zs = lax.rem(z - dz + NZ, NZ)
        return jnp.concatenate([pa[rows_of(ys * NZ + zs), :] for ys in range(4)], 0)

    def gram(left, right):
        return lax.dot_general(left, right, (((0,), (0,)), ((), ())), preferred_element_type=F32)

    places = ((0, 0), (0, H), (H, H))

    def block(site, part):
        at_row, at_lane = places[part]
        return c_all.at[site, pl.ds(at_row, H), pl.ds(at_lane, H)]

    def over_chip(part):
        return pltpu.make_async_remote_copy(
            src_ref=block(s, part),
            dst_ref=block(s, part),
            send_sem=mate_send.at[part],
            recv_sem=mate_recv.at[part],
            device_id={"seg": mate},
            device_id_type=MESH,
        )

    def over_ring(part, d):
        return pltpu.make_async_remote_copy(
            src_ref=block(s, part),
            dst_ref=block(s, part),
            send_sem=ring_send.at[part, d - 1],
            recv_sem=ring_recv.at[part, d - 1],
            device_id={"seg": lax.rem(chip + d, 4) * 2 + core},
            device_id_type=MESH,
        )

    def hand_on(part, d):
        site = lax.rem(chip + 4 - d, 4) * 2 + core
        return pltpu.make_async_remote_copy(
            src_ref=block(site, part),
            dst_ref=block(site, part),
            send_sem=swap_send.at[part, d - 1],
            recv_sem=swap_recv.at[part, d - 1],
            device_id={"seg": mate},
            device_id_type=MESH,
        )

    def give(part):
        for d in (1, 3, 2):
            over_ring(part, d).start()
        over_chip(part).start()

    def relay(part):
        for d in (1, 3, 2):
            over_ring(part, d).wait()
            hand_on(part, d).start()

    def settle(part):
        over_chip(part).wait()
        for d in (1, 3, 2):
            hand_on(part, d).wait()

    for site in range(8):
        c_all[site, H:, :H] = jnp.zeros((H, H), F32)

    w1[:, :H] = jnp.zeros((H, H), F32)
    for dz in [0] + [d * sign for d in range(1, 8) for sign in (1, -1)] + [8]:
        part = collect(0, dz)
        w1[:, :H] += gram(part, part)
    shifted = (row == lane).astype(F32) * (shift_value * shift_value)
    w1[:, :H] = w1[:, :H] * (live_row[0] * live_lane[0] * (1.0 + shift_value)) + shifted
    cholesky(w1)
    c_all[s, :H, :H] = w1[:, :H]
    t11 = w1[:, H:].T

    def both(t):
        high = t.astype(BF16)
        return jnp.concatenate([high, (t - high.astype(F32)).astype(BF16)], 1)

    t1 = both(t11 * live_row[0])

    def first_columns(i, _):
        at_rows = pl.ds(pl.multiple_of(i * B, B), B)
        out = jnp.dot(pa[at_rows, :], t1, preferred_element_type=F32)
        qa[at_rows, :] = (out[:, :H] + out[:, H:]).astype(BF16)
        return 0

    lax.fori_loop(0, 16, first_columns, 0)
    give(0)
    write_a = pltpu.make_async_copy(qa, q_out.at[:, pl.ds(0, H)], out_sem.at[0])
    write_a.start()

    def collect_last(groups):
        for dz in groups:
            part = collect(1, dz)
            c_all[s, :H, H:] += gram(other(dz), part)
            w2[:, :H] += gram(part, part)

    c_all[s, :H, H:] = jnp.zeros((H, H), F32)
    w2[:, :H] = jnp.zeros((H, H), F32)
    collect_last(order_b[:9])
    relay(0)
    settle(0)
    for i in range(4):
        pairs[i, H:, :H] = jnp.zeros((H, H), F32)
        pairs[i, :H, :H] = dot_hi(c_all[2 * i + 1, :H, :H], c_all[2 * i, :H, :H])
    is_even = core == 0

    upper, right, whole = slice(0, H), slice(H, B), slice(0, B)
    acc_out[H:, :H] = jnp.zeros((H, H), F32)

    def last_product(rows, lanes):
        mine = jnp.where(is_even, c_all[s, rows, rows], pairs[chip, rows, rows])

        @pl.when(chip == 0)
        def _():
            acc_out[rows, lanes] = jnp.where(is_even, c_all[s, rows, lanes], pairs[chip, rows, lanes])

        @pl.when(chip > 0)
        def _():
            run[rows, :] = pairs[0, rows, lanes]

        for i in (1, 2):

            @pl.when(chip > i)
            def _():
                run[rows, :] = dot_hi(pairs[i, rows, rows], run[rows, :])

        @pl.when(chip > 0)
        def _():
            acc_out[rows, lanes] = dot_hi(mine, run[rows, :])

    last_product(upper, upper)
    collect_last(order_b[9:] + [0])
    a12 = c_all[s, :H, H:] * (live_row[0] * live_lane[1] * (1.0 + shift_value))
    a22 = w2[:, :H] * (live_row[1] * live_lane[1] * (1.0 + shift_value)) + shifted
    r12 = dot_hi(w1[:, H:], a12)
    c_all[s, :H, H:] = r12
    w2[:, :H] = a22 - transposed_dot(r12, r12)
    mixed = dot_hi(t11, r12)
    give(1)
    cholesky(w2)
    c_all[s, H:, H:] = w2[:, :H]
    t22 = w2[:, H:].T
    t12 = dot_hi(mixed, t22)
    t2 = both(jnp.concatenate([-t12 * live_row[0], t22 * live_row[1]], 0))
    give(2)
    relay(1)

    def last_columns(i, _):
        at_rows = pl.ds(pl.multiple_of(i * B, B), B)
        out = jnp.dot(jnp.concatenate([pa[at_rows, :], pb[at_rows, :]], 1), t2, preferred_element_type=F32)
        qb[at_rows, :] = (out[:, :H] + out[:, H:]).astype(BF16)
        return 0

    lax.fori_loop(0, 16, last_columns, 0)
    write_b = pltpu.make_async_copy(qb, q_out.at[:, pl.ds(H, H)], out_sem.at[1])
    write_b.start()
    settle(1)
    relay(2)
    settle(2)
    for i in range(4):
        pairs[i, :, H:] = dot_hi(c_all[2 * i + 1], c_all[2 * i, :, H:])
    last_product(whole, right)

    for half in (0, 1):
        pltpu.make_async_remote_copy(
            src_ref=x.at[:, pl.ds(0, 63 * H)],
            dst_ref=x.at[:, pl.ds(0, 63 * H)],
            send_sem=send_sem.at[half],
            recv_sem=recv_sem.at[half, 0, 0],
            device_id={"blk": b},
            device_id_type=MESH,
        ).wait_send()
    write_a.wait()
    write_b.wait()


def local(products, compat, sizes):
    vmem, dma = pltpu.VMEM, pltpu.SemaphoreType.DMA
    ortho, acc = pl.pallas_call(
        kernel,
        out_shape=(jax.ShapeDtypeStruct((NY * NZ * ROWS, B), BF16), jax.ShapeDtypeStruct((B, B), F32)),
        in_specs=[
            pl.BlockSpec(memory_space=pltpu.HBM),
            pl.BlockSpec(memory_space=pltpu.HBM),
            pl.BlockSpec(memory_space=pltpu.HBM),
        ],
        out_specs=(pl.BlockSpec(memory_space=pl.ANY), pl.BlockSpec(memory_space=pltpu.VMEM)),
        scratch_shapes=[vmem((NY * NZ * ROWS, H), BF16)] * 4
        + [vmem((H, B), F32)] * 2
        + [vmem((8, B, B), F32), vmem((4, B, B), F32), vmem((B, H), F32)]
        + [
            dma((2,)),
            dma((2, NZ, NY)),
            dma((2,)),
            pltpu.SemaphoreType.REGULAR((2, 8)),
            dma((2,)),
            dma((3,)),
            dma((3,)),
            dma((3, 3)),
            dma((3, 3)),
            dma((3, 3)),
            dma((3, 3)),
            pltpu.SMEM((1, 16), jnp.int32),
            pltpu.SMEM((1, 1), jnp.int32),
            dma((2,)),
        ],
        compiler_params=pltpu.CompilerParams(collective_id=0, has_side_effects=True, vmem_limit_bytes=40 << 20),
        name="sweep",
    )(products[0], compat[0], sizes)
    return ortho[None], acc[None, None]


def solution(mesh):
    in_specs = (P("seg", "blk", None), P("seg", "blk", None), P("seg", "blk"))
    out_specs = (P("seg", None, "blk"), P("seg", "blk", None, None))
    return jax.shard_map(local, mesh=mesh, in_specs=in_specs, out_specs=out_specs, check_vma=False)
```

```python
import jax
import jax.numpy as jnp
from jax import lax
from jax.experimental import pallas as pl
from jax.experimental.pallas import tpu as pltpu
from jax.sharding import PartitionSpec as P

B = 256
H = 128
ROWS = 64
NY, NZ = 4, 16
NB = 8
SUPER = 32
shift_value = 0.05
MESH = pl.DeviceIdType.MESH
HI = lax.Precision.HIGHEST
F32, BF16 = jnp.float32, jnp.bfloat16


def split3(x):
    a = x.astype(BF16)
    rest = x - a.astype(F32)
    b = rest.astype(BF16)
    return a, b, (rest - b.astype(F32)).astype(BF16)


def transposed_dot(x, y):
    xa, xb, xc = split3(x)
    ya, yb, yc = split3(y)
    left = jnp.concatenate([xa, xb, xa, xc, xa, xb], 0)
    right = jnp.concatenate([ya, ya, yb, ya, yc, yb], 0)
    return lax.dot_general(left, right, (((0,), (0,)), ((), ())), preferred_element_type=F32)


def dot_hi(x, y):
    return jnp.dot(x, y, precision=HI, preferred_element_type=F32)


def product(x, y):
    xh, yh = x.astype(BF16), y.astype(BF16)
    xl, yl = (x - xh.astype(F32)).astype(BF16), (y - yh.astype(F32)).astype(BF16)
    left, right = jnp.concatenate([xh, xh, xl], 1), jnp.concatenate([yh, yl, yh], 0)
    return jnp.dot(left, right, preferred_element_type=F32)


def spread(x, r):
    return jnp.broadcast_to(x[r : r + 1, :], (NB, H))


def eliminate(w, v, base):
    groups = len(w)
    row = lax.broadcasted_iota(jnp.int32, (NB, H), 0)
    for g in range(groups):
        first = base + NB * g
        cols = [[jnp.broadcast_to(w[h][:, first + k : first + k + 1], (NB, H)) for k in range(NB)] for h in range(g, groups)]
        pivots = jnp.zeros((NB, H), F32)
        for c in range(NB):
            p = spread(cols[0][c], c)
            pivots = jnp.where(row == c, p, pivots)
            if c == NB - 1 and g == groups - 1:
                break
            q = 1.0 / p
            m = [cols[h - g][c] * q for h in range(g, groups)]
            m[0] = jnp.where(row > c, m[0], 0.0)
            for k in range(c + 1, NB):
                along = spread(cols[0][k], c)
                for h in range(g, groups):
                    cols[h - g][k] = cols[h - g][k] - m[h - g] * along
            w_row, v_row = spread(w[g], c), spread(v[g], c)
            for h in range(g + (c == NB - 1), groups):
                w[h] = w[h] - m[h - g] * w_row
                v[h] = v[h] - m[h - g] * v_row
        root = lax.rsqrt(pivots)
        w[g] = w[g] * root
        v[g] = v[g] * root
    return w, v


def cholesky(work):
    work[:, H:] = (lax.broadcasted_iota(jnp.int32, (H, H), 0) == lax.broadcasted_iota(jnp.int32, (H, H), 1)).astype(F32)
    lane = lax.broadcasted_iota(jnp.int32, (SUPER, H), 1)
    row = lax.broadcasted_iota(jnp.int32, (SUPER, H), 0)
    for start in range(0, H, SUPER):
        end = start + SUPER
        pieces = range(start, end, NB)
        w, v = eliminate([work[i : i + NB, :H] for i in pieces], [work[i : i + NB, H:] for i in pieces], start)
        r = jnp.where(lane >= row + start, jnp.concatenate(w, 0), 0.0)
        rv = jnp.concatenate([r, jnp.concatenate(v, 0)], 1)
        work[start:end, :] = rv
        if end < H:
            work[end:, :] = work[end:, :] - transposed_dot(r, rv)[end:, :]


def kernel(x, compat_in, sizes_in, q_out, acc_out, pa, pb, qa, qb, w1, w2, c_all, pairs, run,
           send_sem, recv_sem, own_sem, wave_sem, out_sem, mate_send, mate_recv, ring_send, ring_recv, swap_send, swap_recv,
           compat, sizes, table_sem):
    b = lax.axis_index("blk")
    s = lax.axis_index("seg")
    y, z = b // NZ, lax.rem(b, NZ)
    chip, core = s // 2, lax.rem(s, 2)
    mate = chip * 2 + 1 - core
    panels = (pa, pb)

    def at(dy, dz):
        return lax.rem(y + dy, NY) * NZ + lax.rem(z + dz + NZ, NZ)

    def rows_of(k):
        return pl.ds(pl.multiple_of(k * ROWS, ROWS), ROWS)

    tables = [
        pltpu.make_async_copy(compat_in, compat, table_sem.at[0]),
        pltpu.make_async_copy(sizes_in, sizes, table_sem.at[1]),
    ]
    for copy in tables:
        copy.start()

    barrier = pltpu.get_barrier_semaphore()
    near = [{"blk": at(dy, 0)} for dy in (1, 2, 3)] + [{"blk": at(0, 1)}, {"blk": at(0, -1)}]
    near += [{"seg": mate}] + [{"seg": lax.rem(chip + d, 4) * 2 + core} for d in (1, 2, 3)]
    for to in near:
        pl.semaphore_signal(barrier, inc=1, device_id=to, device_id_type=MESH)
    pl.semaphore_wait(barrier, len(near))

    def send(half, dy, dz):
        k = at(dy, dz)
        return pltpu.make_async_remote_copy(
            src_ref=x.at[:, pl.ds(pl.multiple_of(k * B + half * H, H), H)],
            dst_ref=panels[half].at[rows_of(b), :],
            send_sem=send_sem.at[half],
            recv_sem=recv_sem.at[half, dz % NZ, dy],
            device_id={"blk": k},
            device_id_type=MESH,
        )

    def arrived(half, dy, dz):
        k = at(NY - dy, -dz)
        pltpu.make_async_remote_copy(
            src_ref=x.at[:, pl.ds(0, H)],
            dst_ref=panels[half].at[rows_of(k), :],
            send_sem=send_sem.at[half],
            recv_sem=recv_sem.at[half, dz % NZ, dy],
            device_id={"blk": k},
            device_id_type=MESH,
        ).wait_recv()

    own = [
        pltpu.make_async_copy(
            x.at[:, pl.ds(pl.multiple_of(b * B + half * H, H), H)], panels[half].at[rows_of(b), :], own_sem.at[half]
        )
        for half in (0, 1)
    ]
    own[0].start()
    own[1].start()

    def tell(direction, hop):
        pl.semaphore_signal(
            wave_sem.at[(1 - direction) // 2, hop - 1],
            inc=1,
            device_id={"blk": at(0, direction)},
            device_id_type=MESH,
        )

    tell(1, 1)
    tell(-1, 1)
    for dy in (1, 2, 3):
        send(0, dy, 0).start()
    for hop in range(1, 9):
        for direction in (1, -1):
            if hop == 8 and direction == -1:
                continue
            pl.semaphore_wait(wave_sem.at[(1 + direction) // 2, hop - 1], 1)
            if hop < 7 or (hop == 7 and direction == 1):
                tell(-direction, hop + 1)
            for dy in range(4):
                send(0, dy, direction * hop).start()
    order_b = [8] + [d * sign for d in range(7, 0, -1) for sign in (1, -1)]
    for dz in order_b:
        for dy in range(4):
            send(1, dy, dz).start()
    for dy in (1, 2, 3):
        send(1, dy, 0).start()

    for copy in tables:
        copy.wait()
    n = sizes[0, 0]
    lane = lax.broadcasted_iota(jnp.int32, (H, H), 1)
    row = lax.broadcasted_iota(jnp.int32, (H, H), 0)
    live_row = [(row < n).astype(F32), (row + H < n).astype(F32)]
    live_lane = [(lane < n).astype(F32), (lane + H < n).astype(F32)]

    def collect(half, dz):
        zs = lax.rem(z - dz + NZ, NZ)
        if dz == 0:
            own[half].wait()
        for dy in range(4):
            if dy or dz:
                arrived(half, dy, dz)
        parts = []
        for ys in range(4):
            k = ys * NZ + zs
            gate = jnp.full((1, H), compat[0, ys * 4 + zs // 4], jnp.int32).astype(F32).astype(BF16)
            part = panels[half][rows_of(k), :] * gate
            panels[half][rows_of(k), :] = part
            parts.append(part)
        return jnp.concatenate(parts, 0)

    def other(dz):
        zs = lax.rem(z - dz + NZ, NZ)
        return jnp.concatenate([pa[rows_of(ys * NZ + zs), :] for ys in range(4)], 0)

    def gram(left, right):
        return lax.dot_general(left, right, (((0,), (0,)), ((), ())), preferred_element_type=F32)

    places = ((0, 0), (0, H), (H, H))

    def block(site, part):
        at_row, at_lane = places[part]
        return c_all.at[site, pl.ds(at_row, H), pl.ds(at_lane, H)]

    def over_chip(part):
        return pltpu.make_async_remote_copy(
            src_ref=block(s, part),
            dst_ref=block(s, part),
            send_sem=mate_send.at[part],
            recv_sem=mate_recv.at[part],
            device_id={"seg": mate},
            device_id_type=MESH,
        )

    def over_ring(part, d):
        return pltpu.make_async_remote_copy(
            src_ref=block(s, part),
            dst_ref=block(s, part),
            send_sem=ring_send.at[part, d - 1],
            recv_sem=ring_recv.at[part, d - 1],
            device_id={"seg": lax.rem(chip + d, 4) * 2 + core},
            device_id_type=MESH,
        )

    def hand_on(part, d):
        site = lax.rem(chip + 4 - d, 4) * 2 + core
        return pltpu.make_async_remote_copy(
            src_ref=block(site, part),
            dst_ref=block(site, part),
            send_sem=swap_send.at[part, d - 1],
            recv_sem=swap_recv.at[part, d - 1],
            device_id={"seg": mate},
            device_id_type=MESH,
        )

    def give(part):
        for d in (1, 3, 2):
            over_ring(part, d).start()
        over_chip(part).start()

    def relay(part):
        for d in (1, 3, 2):
            over_ring(part, d).wait()
            hand_on(part, d).start()

    def settle(part):
        over_chip(part).wait()
        for d in (1, 3, 2):
            hand_on(part, d).wait()

    for site in range(8):
        c_all[site, H:, :H] = jnp.zeros((H, H), F32)

    w1[:, :H] = jnp.zeros((H, H), F32)
    for dz in [0] + [d * sign for d in range(1, 8) for sign in (1, -1)] + [8]:
        part = collect(0, dz)
        w1[:, :H] += gram(part, part)
    shifted = (row == lane).astype(F32) * (shift_value * shift_value)
    w1[:, :H] = w1[:, :H] * (live_row[0] * live_lane[0] * (1.0 + shift_value)) + shifted
    cholesky(w1)
    c_all[s, :H, :H] = w1[:, :H]
    t11 = w1[:, H:].T

    def both(t):
        high = t.astype(BF16)
        return jnp.concatenate([high, (t - high.astype(F32)).astype(BF16)], 1)

    t1 = both(t11 * live_row[0])

    def first_columns(i, _):
        at_rows = pl.ds(pl.multiple_of(i * B, B), B)
        out = jnp.dot(pa[at_rows, :], t1, preferred_element_type=F32)
        qa[at_rows, :] = (out[:, :H] + out[:, H:]).astype(BF16)
        return 0

    lax.fori_loop(0, 16, first_columns, 0)
    give(0)
    write_a = pltpu.make_async_copy(qa, q_out.at[:, pl.ds(0, H)], out_sem.at[0])
    write_a.start()

    def collect_last(groups):
        for dz in groups:
            part = collect(1, dz)
            c_all[s, :H, H:] += gram(other(dz), part)
            w2[:, :H] += gram(part, part)

    c_all[s, :H, H:] = jnp.zeros((H, H), F32)
    w2[:, :H] = jnp.zeros((H, H), F32)
    collect_last(order_b[:9])
    relay(0)
    settle(0)
    for i in range(4):
        pairs[i, H:, :H] = jnp.zeros((H, H), F32)
        pairs[i, :H, :H] = product(c_all[2 * i + 1, :H, :H], c_all[2 * i, :H, :H])
    is_even = core == 0

    upper, right, whole = slice(0, H), slice(H, B), slice(0, B)
    acc_out[H:, :H] = jnp.zeros((H, H), F32)

    def last_product(rows, lanes):
        mine = jnp.where(is_even, c_all[s, rows, rows], pairs[chip, rows, rows])

        @pl.when(chip == 0)
        def _():
            acc_out[rows, lanes] = jnp.where(is_even, c_all[s, rows, lanes], pairs[chip, rows, lanes])

        @pl.when(chip > 0)
        def _():
            run[rows, :] = pairs[0, rows, lanes]

        for i in (1, 2):

            @pl.when(chip > i)
            def _():
                run[rows, :] = product(pairs[i, rows, rows], run[rows, :])

        @pl.when(chip > 0)
        def _():
            acc_out[rows, lanes] = product(mine, run[rows, :])

    last_product(upper, upper)
    collect_last(order_b[9:] + [0])
    a12 = c_all[s, :H, H:] * (live_row[0] * live_lane[1] * (1.0 + shift_value))
    a22 = w2[:, :H] * (live_row[1] * live_lane[1] * (1.0 + shift_value)) + shifted
    r12 = dot_hi(w1[:, H:], a12)
    c_all[s, :H, H:] = r12
    w2[:, :H] = a22 - transposed_dot(r12, r12)
    mixed = dot_hi(t11, r12)
    give(1)
    cholesky(w2)
    c_all[s, H:, H:] = w2[:, :H]
    t22 = w2[:, H:].T
    t12 = dot_hi(mixed, t22)
    t2 = both(jnp.concatenate([-t12 * live_row[0], t22 * live_row[1]], 0))
    give(2)

    def last_columns(i, _):
        at_rows = pl.ds(pl.multiple_of(i * B, B), B)
        out = jnp.dot(jnp.concatenate([pa[at_rows, :], pb[at_rows, :]], 1), t2, preferred_element_type=F32)
        qb[at_rows, :] = (out[:, :H] + out[:, H:]).astype(BF16)
        return 0

    lax.fori_loop(0, 16, last_columns, 0)
    write_b = pltpu.make_async_copy(qb, q_out.at[:, pl.ds(H, H)], out_sem.at[1])
    write_b.start()
    relay(1)
    settle(1)
    for i in range(4):
        pairs[i, :H, H:] = product(c_all[2 * i + 1, :H, :H], c_all[2 * i, :H, H:])
    relay(2)
    settle(2)
    for i in range(4):
        late = product(c_all[2 * i + 1, :, H:], c_all[2 * i, H:, H:])
        pairs[i, :H, H:] += late[:H]
        pairs[i, H:, H:] = late[H:]
    last_product(whole, right)

    for half in (0, 1):
        pltpu.make_async_remote_copy(
            src_ref=x.at[:, pl.ds(0, 63 * H)],
            dst_ref=x.at[:, pl.ds(0, 63 * H)],
            send_sem=send_sem.at[half],
            recv_sem=recv_sem.at[half, 0, 0],
            device_id={"blk": b},
            device_id_type=MESH,
        ).wait_send()
    write_a.wait()
    write_b.wait()


def local(products, compat, sizes):
    vmem, dma = pltpu.VMEM, pltpu.SemaphoreType.DMA
    ortho, acc = pl.pallas_call(
        kernel,
        out_shape=(jax.ShapeDtypeStruct((NY * NZ * ROWS, B), BF16), jax.ShapeDtypeStruct((B, B), F32)),
        in_specs=[
            pl.BlockSpec(memory_space=pltpu.HBM),
            pl.BlockSpec(memory_space=pltpu.HBM),
            pl.BlockSpec(memory_space=pltpu.HBM),
        ],
        out_specs=(pl.BlockSpec(memory_space=pl.ANY), pl.BlockSpec(memory_space=pltpu.VMEM)),
        scratch_shapes=[vmem((NY * NZ * ROWS, H), BF16)] * 4
        + [vmem((H, B), F32)] * 2
        + [vmem((8, B, B), F32), vmem((4, B, B), F32), vmem((B, H), F32)]
        + [
            dma((2,)),
            dma((2, NZ, NY)),
            dma((2,)),
            pltpu.SemaphoreType.REGULAR((2, 8)),
            dma((2,)),
            dma((3,)),
            dma((3,)),
            dma((3, 3)),
            dma((3, 3)),
            dma((3, 3)),
            dma((3, 3)),
            pltpu.SMEM((1, 16), jnp.int32),
            pltpu.SMEM((1, 1), jnp.int32),
            dma((2,)),
        ],
        compiler_params=pltpu.CompilerParams(collective_id=0, has_side_effects=True, vmem_limit_bytes=40 << 20),
        name="sweep",
    )(products[0], compat[0], sizes)
    return ortho[None], acc[None, None]


def solution(mesh):
    in_specs = (P("seg", "blk", None), P("seg", "blk", None), P("seg", "blk"))
    out_specs = (P("seg", None, "blk"), P("seg", "blk", None, None))
    return jax.shard_map(local, mesh=mesh, in_specs=in_specs, out_specs=out_specs, check_vma=False)
```
